32 devices in a mesh: grp: 8 (over y, x, core), sub: 4 (over z).
Axes of the slice: x: 2, y: 2, z: 4, core: 2. Of those that a mesh axis runs over, the one named last changes fastest.
Arguments:
- basis: bfloat16 [8, 4, 270, 1152], P('grp', 'sub'), may hold values from -6 to 6
- stiffness: bfloat16 [8, 4, 1152, 1152], P('grp', 'sub'), may hold values from -0.1875 to 0.1875
- inverse: bfloat16 [8, 4, 1152, 1152], P('grp', 'sub'), may hold values from -0.1875 to 0.1875
- coupling: bfloat16 [8, 4, 4, 768, 1152], P('grp', 'sub'), may hold values from -0.109375 to 0.109375
- panel_index: int32 [8, 4, 4, 6], P('grp', 'sub'), may hold values from 0 to 8, as said below
- panel_count: int32 [8, 4, 4], P('grp', 'sub'), may hold values from 1 to 6, as said below
- owner_map: int32 [8, 4, 270], P('grp', 'sub'), may hold values from 0 to 255, as said below
Outputs:
- coarse_matrix: float32 [256, 256], P(('grp', 'sub'))
The draws below stay inside these ranges and needn't reach their ends.
Inputs may be any that keep to these rules, and one draw needn't show every extreme that they name: `panel_index`: in every draw some slot names panel 9 - 1 and some names panel 0. `panel_count`: in every draw some direction has 6 live slots and some has one. Subdomain (g, s) owns the rows b * 8 to b * 8 + 7 of coarse_matrix with b = g * 4 + s; entries of owner_map may name any column, repeats allowed; column 0 and column 256 - 1 are named in every draw.
All inputs are finite; a program needn't handle non-finite values.
Results may differ from the reference program's by a relative error of at most 0.0056.
Values may be sent and summed in bfloat16 or wider, within the bound.
No kernel may reach another device: no remote copies, remote signals or barrier semaphores. Data moves between devices by JAX's collectives and lax.ppermute only.
A program may use at most 128 MiB of HBM per device.

```python
import jax
import jax.numpy as jnp
from jax import lax

K = 270
PANEL = 128
NB = 9
CMAX = 6
OWN = 8
N_GRP = 8
N_SUB = 4


def draw_panel_index(key, part):
    drawn = jax.random.randint(key, (N_GRP, N_SUB, 4, CMAX), 0, NB)
    return drawn.at[0, 0, 0, 0].set(NB - 1).at[0, 0, 1, 0].set(0)


def draw_panel_count(key, part):
    drawn = jax.random.randint(jax.random.fold_in(key, 7), (N_GRP, N_SUB, 4), 1, CMAX + 1)
    return drawn.at[0, 0, 0].set(CMAX).at[0, 0, 1].set(1)


def draw_owner_map(key, part):
    owners = jax.random.randint(jax.random.fold_in(key, 11), (N_GRP, N_SUB, K), 0, OWN * N_GRP * N_SUB)
    owners = owners.at[0, 0, 0].set(0).at[N_GRP - 1, N_SUB - 1, 0].set(OWN * N_GRP * N_SUB - 1)
    return owners.astype(jnp.int32)


def levels(key, extent, cuts, smallest, high):
    def one(dim, blocks):
        heights = jax.random.uniform(jax.random.fold_in(jax.random.fold_in(key, 6), dim), (blocks,), jnp.float32, smallest / len(cuts), high / len(cuts))
        return jnp.repeat(jnp.exp(heights), extent[dim] // blocks).reshape((-1,) + (1,) * (len(extent) - dim - 1))

    gain = one(*cuts[0])
    for cut in cuts[1:]:
        gain = gain * one(*cut)
    return gain


def scatter_about(own_key, extent, width, limit, shards=(), kind=jnp.bfloat16):
    values = width * jax.random.normal(own_key, extent, jnp.float32)
    if shards:
        values = values * levels(own_key, extent, shards, -0.22, 0.18)
    return jnp.clip(values, -limit, limit).astype(kind)


def setup_inputs(seed: int = 0) -> dict:
    arg_keys = jax.random.split(jax.random.key(seed), 8)
    basis = scatter_about(arg_keys[0], (N_GRP, N_SUB, K, NB * PANEL), 1.0, 6.0, ((0, 8), (1, 4)))
    stiffness = scatter_about(arg_keys[1], (N_GRP, N_SUB, NB * PANEL, NB * PANEL), (NB * PANEL) ** -0.5, 0.1875, ((0, 8), (1, 4)))
    inverse = scatter_about(arg_keys[2], (N_GRP, N_SUB, NB * PANEL, NB * PANEL), (NB * PANEL) ** -0.5, 0.1875, ((0, 8), (1, 4)))
    coupling = scatter_about(arg_keys[3], (N_GRP, N_SUB, 4, CMAX * PANEL, NB * PANEL), (4 * CMAX * PANEL) ** -0.5, 0.109375, ((0, 8), (1, 4)))
    panel_index = draw_panel_index(jax.random.fold_in(arg_keys[7], 71), 0)
    panel_count = draw_panel_count(jax.random.fold_in(arg_keys[7], 71), 0)
    owner_map = draw_owner_map(jax.random.fold_in(arg_keys[7], 71), 0)
    return dict(basis=basis, stiffness=stiffness, inverse=inverse, coupling=coupling, panel_index=panel_index, panel_count=panel_count, owner_map=owner_map)


def pick_panels(values, panel_ids, live_count):
    panels = values.reshape(values.shape[0], NB, PANEL)
    chosen = jnp.take(panels, panel_ids.astype(jnp.int32), axis=1)
    alive_mask = (jnp.arange(CMAX) < live_count).astype(values.dtype)
    return chosen * alive_mask[None, :, None]


def extend(basis, neighbours, stiffness, inverse, coupling, panel_index, panel_count):
    picked = [pick_panels(neighbours[direction], panel_index[direction], panel_count[direction]) for direction in range(4)]
    rows_margin = jnp.stack(picked, axis=1).reshape(K, 4 * CMAX * PANEL)
    margin = jnp.dot(rows_margin, coupling.reshape(4 * CMAX * PANEL, NB * PANEL), preferred_element_type=jnp.float32).astype(jnp.bfloat16)
    extension = (jnp.dot(basis, inverse, preferred_element_type=jnp.float32) + jnp.dot(margin, inverse, preferred_element_type=jnp.float32)).astype(jnp.bfloat16)
    projected = jnp.dot(extension, stiffness, preferred_element_type=jnp.float32).astype(jnp.bfloat16)
    scale_factor = float(NB * PANEL * K) ** -0.5
    return jnp.dot(projected, extension.T, preferred_element_type=jnp.float32) * scale_factor


def reference(basis, stiffness, inverse, coupling, panel_index, panel_count, owner_map):
    padded = jnp.pad(basis, ((1, 1), (1, 1), (0, 0), (0, 0)))
    neighbours = jnp.stack([padded[:-2, 1:-1], padded[2:, 1:-1], padded[1:-1, :-2], padded[1:-1, 2:]], axis=2)
    devices_all = N_GRP * N_SUB
    device_items = (
        basis.reshape(devices_all, K, NB * PANEL),
        neighbours.reshape(devices_all, 4, K, NB * PANEL),
        stiffness.reshape(devices_all, NB * PANEL, NB * PANEL),
        inverse.reshape(devices_all, NB * PANEL, NB * PANEL),
        coupling.reshape(devices_all, 4, CMAX * PANEL, NB * PANEL),
        panel_index.reshape(devices_all, 4, CMAX),
        panel_count.reshape(devices_all, 4),
        owner_map.reshape(devices_all, K),
    )

    def accumulate(running, items):
        coarse = extend(items[0], items[1], items[2], items[3], items[4], items[5], items[6])
        owners = items[7].astype(jnp.int32)
        return running.at[owners[:, None], owners[None, :]].add(coarse), None

    running = jnp.zeros((OWN * N_GRP * N_SUB, OWN * N_GRP * N_SUB), jnp.float32)
    running, unused = lax.scan(accumulate, running, device_items)
    return running
```

```python
import jax
import jax.numpy as jnp
from jax import lax
from jax.experimental import pallas as pl
from jax.experimental.pallas import tpu as pltpu
from jax.sharding import PartitionSpec as P

PANEL = 128
F32 = jnp.float32
BF16 = jnp.bfloat16


def swaps(count):
    even = [(i, i + 1) for i in range(0, count - 1, 2)]
    odd = [(i, i + 1) for i in range(1, count - 1, 2)]
    return [both + [(b, a) for a, b in both] for both in (even, odd)]


def split_dot(table, values, contract):
    high = values.astype(BF16)
    low = (values - high.astype(F32)).astype(BF16)
    dims = (contract, ((), ()))
    return lax.dot_general(table, high, dims, preferred_element_type=F32) + lax.dot_general(
        table, low, dims, preferred_element_type=F32
    )


def subdomain_kernel(
    scale, index_ref, count_ref, owner_ref, first_ref, even_sub, odd_sub, odd_grp, even_grp,
    coupling_ref, inverse_ref, stiffness_ref, out_ref, picked, margin,
):
    columns = even_sub.shape[0]
    slots = index_ref.shape[-1]
    grp_odd = lax.rem(lax.axis_index("grp"), 2)
    sub_odd = lax.rem(lax.axis_index("sub"), 2)
    arrivals = (
        (even_sub, 3 - sub_odd),
        (odd_sub, 2 + sub_odd),
        (odd_grp, grp_odd),
        (even_grp, 1 - grp_odd),
    )
    for number, (values, direction) in enumerate(arrivals):
        live = count_ref[0, 0, direction]
        for slot in range(slots):
            place = index_ref[0, 0, direction, slot]
            panel = values[:, pl.ds(pl.multiple_of(place * PANEL, PANEL), PANEL)]
            alive = jnp.where(slot < live, 1.0, 0.0).astype(BF16)
            picked[:, slot * PANEL : (slot + 1) * PANEL] = panel * alive
        product = jnp.dot(picked[...], coupling_ref[direction], preferred_element_type=F32)
        if number == 0:
            margin[...] = product
        else:
            margin[...] += product
    extension = (
        first_ref[...]
        + jnp.dot(margin[...].astype(BF16), inverse_ref[...], preferred_element_type=F32)
    ).astype(BF16)
    projected = jnp.dot(extension, stiffness_ref[...], preferred_element_type=F32).astype(BF16)
    last = ((1,), (1,))
    coarse = (
        lax.dot_general(projected, extension, (last, ((), ())), preferred_element_type=F32) * scale
    )
    places = lax.broadcasted_iota(jnp.int32, (out_ref.shape[0], columns), 0)
    table = (owner_ref[0] == places).astype(F32).astype(BF16)
    turned = split_dot(table, coarse, last)
    out_ref[...] = split_dot(table, turned, last).astype(out_ref.dtype)


def shards(basis, stiffness, inverse, coupling, panel_index, panel_count, owner_map):
    basis, stiffness, inverse, coupling = (a[0, 0] for a in (basis, stiffness, inverse, coupling))
    columns, rows = basis.shape
    blocks = lax.axis_size("grp") * lax.axis_size("sub")
    own = 8
    columns_all = own * blocks
    even_sub, odd_sub = swaps(lax.axis_size("sub"))
    even_grp, odd_grp = swaps(lax.axis_size("grp"))
    from_even_grp = lax.ppermute(basis, "grp", even_grp)
    from_odd_grp = lax.ppermute(basis, "grp", odd_grp)
    from_odd_sub = lax.ppermute(basis, "sub", odd_sub)
    from_even_sub = lax.ppermute(basis, "sub", even_sub)
    first = jnp.dot(basis, inverse, preferred_element_type=F32)
    vmem = pl.BlockSpec(memory_space=pltpu.VMEM)
    smem = pl.BlockSpec(memory_space=pltpu.SMEM)
    scale = float(rows * columns) ** -0.5
    flops = 2 * columns * rows * (coupling.shape[0] * coupling.shape[1] + 2 * rows + columns)
    contributions = pl.pallas_call(
        lambda *refs: subdomain_kernel(scale, *refs),
        out_shape=jax.ShapeDtypeStruct((columns_all, columns_all), BF16),
        in_specs=[smem, smem] + [vmem] * 9,
        out_specs=vmem,
        scratch_shapes=[
            pltpu.VMEM((columns, coupling.shape[1]), BF16),
            pltpu.VMEM((columns, rows), F32),
        ],
        cost_estimate=pl.CostEstimate(flops=flops, bytes_accessed=12 * 2**20, transcendentals=0),
    )(
        panel_index, panel_count, owner_map, first,
        from_even_sub, from_odd_sub, from_odd_grp, from_even_grp,
        coupling, inverse, stiffness,
    )
    parts = lax.all_to_all(
        contributions.reshape(blocks, own, columns_all), ("grp", "sub"), 0, 0, tiled=True
    )
    return jnp.sum(parts.astype(F32), axis=0)


def solution(mesh):
    three, four = P("grp", "sub", None), P("grp", "sub", None, None)
    in_specs = (four, four, four, P("grp", "sub", None, None, None), four, three, three)
    out_specs = P(("grp", "sub"), None)
    return jax.shard_map(shards, mesh=mesh, in_specs=in_specs, out_specs=out_specs, check_vma=False)
```

```python
import jax
import jax.numpy as jnp
import numpy as np
from jax import lax
from jax.experimental import pallas as pl
from jax.experimental.pallas import tpu as pltpu
from jax.sharding import PartitionSpec as P

PANEL = 128
OWN = 8
F32 = jnp.float32
BF16 = jnp.bfloat16
EARLY, MIDDLE, LATE = 3, (0,), (1, 2)
ORDER = (0, 1, 2, 3)
VMEM = pl.BlockSpec(memory_space=pltpu.VMEM)
SMEM = pl.BlockSpec(memory_space=pltpu.SMEM)


def exchange_rounds(groups, members):
    rounds = [[], [], [], []]
    for g in range(groups):
        inner = g % 4 in (1, 2)
        across = g + 1 < groups if g % 2 else g > 0
        turns = ("BXA" if inner else "ABX") if across else "AB"
        for s in range(members - 1):
            rounds[turns.index("BA"[s % 2 == 0])].append(((g, s), (g, s + 1)))
        if g + 1 < groups:
            for s in range(members):
                if g % 2 == 0:
                    number = 3
                elif s == 0 or s == members - 1 and s % 2:
                    number = min({0, 1, 2} - {turns.index("A")})
                else:
                    number = turns.index("X")
                rounds[number].append(((g, s), (g + 1, s)))
    sources = np.full((groups * members, len(rounds)), -1, np.int32)
    swaps = []
    for number, pairs in enumerate(rounds):
        flat = []
        for low, high in pairs:
            a, b = (g * members + s for g, s in (low, high))
            along_sub = low[0] == high[0]
            assert max(sources[a, number], sources[b, number]) < 0
            sources[a, number] = 3 if along_sub else 1
            sources[b, number] = 2 if along_sub else 0
            flat += [(a, b), (b, a)]
        swaps.append(flat)
    return swaps, sources


def margin_product(number, me, source_ref, index_ref, count_ref, values, coupling_ref, picked):
    source = source_ref[me, number]
    direction = jnp.maximum(source, 0)
    live = count_ref[0, 0, direction]
    for slot in range(index_ref.shape[-1]):
        place = index_ref[0, 0, direction, slot]
        panel = values[:, pl.ds(pl.multiple_of(place * PANEL, PANEL), PANEL)]
        alive = jnp.where(slot < live, 1.0, 0.0).astype(BF16)
        picked[:, slot * PANEL : (slot + 1) * PANEL] = panel * alive
    return jnp.dot(picked[...], coupling_ref[direction], preferred_element_type=F32)


def place_of():
    return lax.axis_index("grp") * lax.axis_size("sub") + lax.axis_index("sub")


def early_kernel(
    number, source_ref, index_ref, count_ref, owner_ref, values, coupling_ref,
    out_ref, table_ref, turned_ref, picked,
):
    out_ref[...] = margin_product(
        number, place_of(), source_ref, index_ref, count_ref, values, coupling_ref, picked
    )
    places = lax.broadcasted_iota(jnp.int32, table_ref.shape, 0)
    table = (owner_ref[0] == places).astype(F32)
    table_ref[...] = table.astype(BF16)
    turned_ref[...] = table.T.astype(BF16)


def next_kernel(number, source_ref, index_ref, count_ref, values, coupling_ref, so_far, out_ref, picked):
    out_ref[...] = so_far[...] + margin_product(
        number, place_of(), source_ref, index_ref, count_ref, values, coupling_ref, picked
    )


def last_kernel(
    numbers, scale, source_ref, index_ref, count_ref, table_ref, turned_ref, first_ref, so_far, *refs
):
    arrived = refs[: len(numbers)]
    coupling_ref, inverse_ref, stiffness_ref, out_ref, picked, margin = refs[len(numbers) :]
    columns = margin.shape[0]
    me = place_of()
    for at, (number, values) in enumerate(zip(numbers, arrived)):
        product = margin_product(
            number, me, source_ref, index_ref, count_ref, values, coupling_ref, picked
        )
        margin[...] = (so_far if at == 0 else margin)[...] + product
    extension = (
        first_ref[...]
        + jnp.dot(margin[...].astype(BF16), inverse_ref[...], preferred_element_type=F32)
    ).astype(BF16)
    projected = jnp.dot(extension, stiffness_ref[...], preferred_element_type=F32).astype(BF16)
    coarse = lax.dot_general(
        projected, extension, (((1,), (1,)), ((), ())), preferred_element_type=F32
    )
    coarse = (coarse * scale).astype(BF16)
    placed = jnp.dot(table_ref[...], coarse, preferred_element_type=F32).astype(BF16)
    out_ref[...] = jnp.dot(placed, turned_ref[...], preferred_element_type=F32).astype(BF16)


def shards(swaps, sources, basis, stiffness, inverse, coupling, panel_index, panel_count, owner_map):
    basis, stiffness, inverse, coupling = (a[0, 0] for a in (basis, stiffness, inverse, coupling))
    columns, rows = basis.shape
    blocks = lax.axis_size("grp") * lax.axis_size("sub")
    columns_all = OWN * blocks
    arrivals = [None] * len(swaps)
    for number in ORDER:
        arrivals[number] = lax.ppermute(basis, ("grp", "sub"), swaps[number])
    first = jnp.dot(basis, inverse, preferred_element_type=F32)
    coupling, inverse, stiffness = (
        pltpu.with_memory_space_constraint(a, pltpu.VMEM) for a in (coupling, inverse, stiffness)
    )
    tables = (jnp.asarray(sources), panel_index, panel_count)
    scale = float(rows * columns) ** -0.5
    slots_wide = coupling.shape[1]
    picked = pltpu.VMEM((columns, slots_wide), BF16)
    step = 2 * columns * slots_wide * rows
    room = 8 * 2**20 + 4 * columns_all**2
    params = pltpu.CompilerParams(vmem_limit_bytes=room)
    margin, table, turned = pl.pallas_call(
        lambda *refs: early_kernel(EARLY, *refs),
        out_shape=(
            jax.ShapeDtypeStruct((columns, rows), F32),
            jax.ShapeDtypeStruct((columns_all, columns), BF16),
            jax.ShapeDtypeStruct((columns, columns_all), BF16),
        ),
        in_specs=[SMEM] * 3 + [VMEM] * 3,
        out_specs=(VMEM,) * 3,
        scratch_shapes=[picked],
        cost_estimate=pl.CostEstimate(flops=step, bytes_accessed=3 * 2**20, transcendentals=0),
        compiler_params=params,
    )(*tables, owner_map, arrivals[EARLY], coupling)
    for number in MIDDLE:
        margin = pl.pallas_call(
            lambda *refs, number=number: next_kernel(number, *refs),
            out_shape=jax.ShapeDtypeStruct((columns, rows), F32),
            in_specs=[SMEM] * 3 + [VMEM] * 3,
            out_specs=VMEM,
            scratch_shapes=[picked],
            cost_estimate=pl.CostEstimate(flops=step, bytes_accessed=3 * 2**20, transcendentals=0),
            compiler_params=params,
        )(*tables, arrivals[number], coupling, margin)
    contributions = pl.pallas_call(
        lambda *refs: last_kernel(LATE, scale, *refs),
        out_shape=jax.ShapeDtypeStruct((columns_all, columns_all), BF16),
        in_specs=[SMEM] * 3 + [VMEM] * (7 + len(LATE)),
        out_specs=VMEM,
        scratch_shapes=[picked, pltpu.VMEM((columns, rows), F32)],
        cost_estimate=pl.CostEstimate(
            flops=step * len(LATE) + 2 * columns * rows * (2 * rows + columns),
            bytes_accessed=12 * 2**20,
            transcendentals=0,
        ),
        compiler_params=params,
    )(*tables, table, turned, first, margin, *(arrivals[n] for n in LATE), coupling, inverse, stiffness)
    parts = lax.all_to_all(
        contributions.reshape(blocks, OWN, columns_all), ("grp", "sub"), 0, 0, tiled=True
    )
    return jnp.sum(parts.astype(F32), axis=0)


def solution(mesh):
    three, four = P("grp", "sub", None), P("grp", "sub", None, None)
    in_specs = (four, four, four, P("grp", "sub", None, None, None), four, three, three)
    out_specs = P(("grp", "sub"), None)
    swaps, sources = exchange_rounds(mesh.shape["grp"], mesh.shape["sub"])
    return jax.shard_map(
        lambda *args: shards(swaps, sources, *args),
        mesh=mesh, in_specs=in_specs, out_specs=out_specs, check_vma=False,
    )
```

```python
import jax
import jax.numpy as jnp
import numpy as np
from jax import lax
from jax.experimental import pallas as pl
from jax.experimental.pallas import tpu as pltpu
from jax.sharding import PartitionSpec as P

PANEL = 128
OWN = 8
F32 = jnp.float32
BF16 = jnp.bfloat16
MIDDLE, LATE = (3, 0, 1), (2,)
ORDER = (0, 1, 2, 3)
VMEM = pl.BlockSpec(memory_space=pltpu.VMEM)
SMEM = pl.BlockSpec(memory_space=pltpu.SMEM)
HBM = pl.BlockSpec(memory_space=pltpu.HBM)


def exchange_rounds(groups, members):
    rounds = [[], [], [], []]
    for g in range(groups):
        inner = g % 4 in (1, 2)
        across = g + 1 < groups if g % 2 else g > 0
        turns = ("BXA" if inner else "ABX") if across else "AB"
        for s in range(members - 1):
            rounds[turns.index("BA"[s % 2 == 0])].append(((g, s), (g, s + 1)))
        if g + 1 < groups:
            for s in range(members):
                if g % 2 == 0:
                    number = 3
                elif s == 0 or s == members - 1 and s % 2:
                    number = min({0, 1, 2} - {turns.index("A")})
                else:
                    number = turns.index("X")
                rounds[number].append(((g, s), (g + 1, s)))
    sources = np.full((groups * members, len(rounds)), -1, np.int32)
    swaps = []
    for number, pairs in enumerate(rounds):
        flat = []
        for low, high in pairs:
            a, b = (g * members + s for g, s in (low, high))
            along_sub = low[0] == high[0]
            assert max(sources[a, number], sources[b, number]) < 0
            sources[a, number] = 3 if along_sub else 1
            sources[b, number] = 2 if along_sub else 0
            flat += [(a, b), (b, a)]
        swaps.append(flat)
    return swaps, sources


def margin_product(number, me, source_ref, index_ref, count_ref, values, coupling_ref, picked):
    source = source_ref[me, number]
    direction = jnp.maximum(source, 0)
    live = count_ref[0, 0, direction]
    for slot in range(index_ref.shape[-1]):
        place = index_ref[0, 0, direction, slot]
        panel = values[:, pl.ds(pl.multiple_of(place * PANEL, PANEL), PANEL)]
        alive = jnp.where(slot < live, 1.0, 0.0).astype(BF16)
        picked[:, slot * PANEL : (slot + 1) * PANEL] = panel * alive
    return jnp.dot(picked[...], coupling_ref[direction], preferred_element_type=F32)


def place_of():
    return lax.axis_index("grp") * lax.axis_size("sub") + lax.axis_index("sub")


def early_kernel(
    owner_ref, basis_hbm, inverse_hbm, coupling_hbm, stiffness_hbm,
    first_ref, table_ref, turned_ref, inverse_ref, coupling_ref, stiffness_ref,
    basis_ref, arrived,
):
    copies = [
        pltpu.make_async_copy(source, target, arrived.at[at])
        for at, (source, target) in enumerate(
            (
                (basis_hbm, basis_ref),
                (inverse_hbm, inverse_ref),
                (coupling_hbm, coupling_ref),
                (stiffness_hbm, stiffness_ref),
            )
        )
    ]
    for copy in copies:
        copy.start()
    places = lax.broadcasted_iota(jnp.int32, table_ref.shape, 0)
    table = (owner_ref[0] == places).astype(F32)
    table_ref[...] = table.astype(BF16)
    turned_ref[...] = table.T.astype(BF16)
    copies[0].wait()
    copies[1].wait()
    first_ref[...] = jnp.dot(basis_ref[...], inverse_ref[...], preferred_element_type=F32)
    copies[2].wait()
    copies[3].wait()


def margin_kernel(number, source_ref, index_ref, count_ref, values, coupling_ref, *refs):
    *so_far, out_ref, picked = refs
    product = margin_product(
        number, place_of(), source_ref, index_ref, count_ref, values, coupling_ref, picked
    )
    out_ref[...] = so_far[0][...] + product if so_far else product


def last_kernel(
    numbers, scale, source_ref, index_ref, count_ref, table_ref, turned_ref, first_ref, so_far, *refs
):
    arrived = refs[: len(numbers)]
    coupling_ref, inverse_ref, stiffness_ref, out_ref, picked, margin = refs[len(numbers) :]
    columns = margin.shape[0]
    me = place_of()
    for at, (number, values) in enumerate(zip(numbers, arrived)):
        product = margin_product(
            number, me, source_ref, index_ref, count_ref, values, coupling_ref, picked
        )
        margin[...] = (so_far if at == 0 else margin)[...] + product
    extension = (
        first_ref[...]
        + jnp.dot(margin[...].astype(BF16), inverse_ref[...], preferred_element_type=F32)
    ).astype(BF16)
    projected = jnp.dot(extension, stiffness_ref[...], preferred_element_type=F32).astype(BF16)
    coarse = lax.dot_general(
        projected, extension, (((1,), (1,)), ((), ())), preferred_element_type=F32
    )
    coarse = (coarse * scale).astype(BF16)
    placed = jnp.dot(table_ref[...], coarse, preferred_element_type=F32).astype(BF16)
    out_ref[...] = jnp.dot(placed, turned_ref[...], preferred_element_type=F32).astype(BF16)


def shards(swaps, sources, basis, stiffness, inverse, coupling, panel_index, panel_count, owner_map):
    basis, stiffness, inverse, coupling = (a[0, 0] for a in (basis, stiffness, inverse, coupling))
    columns, rows = basis.shape
    blocks = lax.axis_size("grp") * lax.axis_size("sub")
    columns_all = OWN * blocks
    arrivals = [None] * len(swaps)
    for number in ORDER:
        arrivals[number] = lax.ppermute(basis, ("grp", "sub"), swaps[number])
    stay = lambda *arrays: tuple(pltpu.with_memory_space_constraint(a, pltpu.HBM) for a in arrays)
    tables = stay(jnp.asarray(sources), panel_index, panel_count)
    scale = float(rows * columns) ** -0.5
    slots_wide = coupling.shape[1]
    picked = pltpu.VMEM((columns, slots_wide), BF16)
    step = 2 * columns * slots_wide * rows
    room = 8 * 2**20 + 4 * columns_all**2
    params = pltpu.CompilerParams(vmem_limit_bytes=room)
    whole = jax.ShapeDtypeStruct((columns, rows), F32)
    first, table, turned, inverse, coupling, stiffness = pl.pallas_call(
        early_kernel,
        out_shape=(
            whole,
            jax.ShapeDtypeStruct((columns_all, columns), BF16),
            jax.ShapeDtypeStruct((columns, columns_all), BF16),
            *(jax.ShapeDtypeStruct(a.shape, BF16) for a in (inverse, coupling, stiffness)),
        ),
        in_specs=[VMEM] + [HBM] * 4,
        out_specs=(VMEM,) * 6,
        scratch_shapes=[
            pltpu.VMEM((columns, rows), BF16), pltpu.SemaphoreType.DMA((4,))
        ],
        cost_estimate=pl.CostEstimate(
            flops=2 * columns * rows * rows, bytes_accessed=26 * 2**20, transcendentals=0
        ),
        compiler_params=pltpu.CompilerParams(vmem_limit_bytes=room + 16 * 2**20),
    )(*stay(owner_map, basis, inverse, coupling, stiffness))
    margin = ()
    for number in MIDDLE:
        margin = (
            pl.pallas_call(
                lambda *refs, number=number: margin_kernel(number, *refs),
                out_shape=whole,
                in_specs=[SMEM] * 3 + [VMEM] * (2 + len(margin)),
                out_specs=VMEM,
                scratch_shapes=[picked],
                cost_estimate=pl.CostEstimate(
                    flops=step, bytes_accessed=3 * 2**20, transcendentals=0
                ),
                compiler_params=params,
            )(*tables, arrivals[number], coupling, *margin),
        )
    contributions = pl.pallas_call(
        lambda *refs: last_kernel(LATE, scale, *refs),
        out_shape=jax.ShapeDtypeStruct((columns_all, columns_all), BF16),
        in_specs=[SMEM] * 3 + [VMEM] * (7 + len(LATE)),
        out_specs=VMEM,
        scratch_shapes=[picked, pltpu.VMEM((columns, rows), F32)],
        cost_estimate=pl.CostEstimate(
            flops=step * len(LATE) + 2 * columns * rows * (2 * rows + columns),
            bytes_accessed=12 * 2**20,
            transcendentals=0,
        ),
        compiler_params=params,
    )(*tables, table, turned, first, *margin, *(arrivals[n] for n in LATE), coupling, inverse, stiffness)
    parts = lax.all_to_all(
        contributions.reshape(blocks, OWN, columns_all), ("grp", "sub"), 0, 0, tiled=True
    )
    return jnp.sum(parts.astype(F32), axis=0)


def solution(mesh):
    three, four = P("grp", "sub", None), P("grp", "sub", None, None)
    in_specs = (four, four, four, P("grp", "sub", None, None, None), four, three, three)
    out_specs = P(("grp", "sub"), None)
    swaps, sources = exchange_rounds(mesh.shape["grp"], mesh.shape["sub"])
    return jax.shard_map(
        lambda *args: shards(swaps, sources, *args),
        mesh=mesh, in_specs=in_specs, out_specs=out_specs, check_vma=False,
    )
```

```python
import jax
import jax.numpy as jnp
import numpy as np
from jax import lax
from jax.experimental import pallas as pl
from jax.experimental.pallas import tpu as pltpu
from jax.sharding import PartitionSpec as P

PANEL = 128
OWN = 8
F32 = jnp.float32
BF16 = jnp.bfloat16
MIDDLE, LATE = (3, 0, 1), (2,)
ORDER = (0, 1, 2, 3)
VMEM = pl.BlockSpec(memory_space=pltpu.VMEM)
SMEM = pl.BlockSpec(memory_space=pltpu.SMEM)
HBM = pl.BlockSpec(memory_space=pltpu.HBM)


def exchange_rounds(groups, members):
    rounds = [[], [], [], []]
    for g in range(groups):
        inner = g % 4 in (1, 2)
        across = g + 1 < groups if g % 2 else g > 0
        turns = ("BXA" if inner else "ABX") if across else "AB"
        for s in range(members - 1):
            rounds[turns.index("BA"[s % 2 == 0])].append(((g, s), (g, s + 1)))
        if g + 1 < groups:
            for s in range(members):
                if g % 2 == 0:
                    number = 3
                elif s == 0 or s == members - 1 and s % 2:
                    number = min({0, 1, 2} - {turns.index("A")})
                else:
                    number = turns.index("X")
                rounds[number].append(((g, s), (g + 1, s)))
    sources = np.full((groups * members, len(rounds)), -1, np.int32)
    swaps = []
    for number, pairs in enumerate(rounds):
        flat = []
        for low, high in pairs:
            a, b = (g * members + s for g, s in (low, high))
            along_sub = low[0] == high[0]
            assert max(sources[a, number], sources[b, number]) < 0
            sources[a, number] = 3 if along_sub else 1
            sources[b, number] = 2 if along_sub else 0
            flat += [(a, b), (b, a)]
        swaps.append(flat)
    return swaps, sources


def packing(panels, slots):
    bits, count_bits = (panels - 1).bit_length(), slots.bit_length()
    assert slots * bits + count_bits + 2 < 32
    return bits, count_bits


def margin_product(number, plan_ref, values, coupling_ref, picked):
    slots = picked.shape[1] // PANEL
    bits, count_bits = packing(values.shape[1] // PANEL, slots)
    plan = plan_ref[0, number]
    direction = plan & 3
    live = (plan >> 2) & (2**count_bits - 1)
    for slot in range(slots):
        place = (plan >> (2 + count_bits + slot * bits)) & (2**bits - 1)
        panel = values[:, pl.ds(pl.multiple_of(place * PANEL, PANEL), PANEL)]
        alive = jnp.where(slot < live, 1.0, 0.0).astype(BF16)
        picked[:, slot * PANEL : (slot + 1) * PANEL] = panel * alive
    return jnp.dot(picked[...], coupling_ref[direction], preferred_element_type=F32)


def write_plans(source_ref, index_ref, count_ref, panels, plan_ref):
    slots = index_ref.shape[-1]
    bits, count_bits = packing(panels, slots)
    me = place_of()
    at = lax.broadcasted_iota(jnp.int32, plan_ref.shape, 1)
    plans = jnp.zeros(plan_ref.shape, jnp.int32)
    for number in range(source_ref.shape[1]):
        source = source_ref[me, number]
        direction = jnp.maximum(source, 0)
        plan = direction + jnp.where(source < 0, 0, count_ref[0, 0, direction]) * 4
        for slot in range(slots):
            plan += index_ref[0, 0, direction, slot] << (2 + count_bits + slot * bits)
        plans = jnp.where(at == number, plan, plans)
    plan_ref[...] = plans


def place_of():
    return lax.axis_index("grp") * lax.axis_size("sub") + lax.axis_index("sub")


def early_kernel(
    source_ref, index_ref, count_ref, owner_ref, basis_hbm, inverse_hbm, coupling_hbm, stiffness_hbm,
    plan_ref, first_ref, table_ref, turned_ref, inverse_ref, coupling_ref, stiffness_ref,
    basis_ref, arrived,
):
    copies = [
        pltpu.make_async_copy(source, target, arrived.at[at])
        for at, (source, target) in enumerate(
            (
                (basis_hbm, basis_ref),
                (inverse_hbm, inverse_ref),
                (coupling_hbm, coupling_ref),
                (stiffness_hbm, stiffness_ref),
            )
        )
    ]
    for copy in copies:
        copy.start()
    write_plans(source_ref, index_ref, count_ref, basis_ref.shape[1] // PANEL, plan_ref)
    places = lax.broadcasted_iota(jnp.int32, table_ref.shape, 0)
    table = (owner_ref[0] == places).astype(F32)
    table_ref[...] = table.astype(BF16)
    turned_ref[...] = table.T.astype(BF16)
    copies[0].wait()
    copies[1].wait()
    first_ref[...] = jnp.dot(basis_ref[...], inverse_ref[...], preferred_element_type=F32)
    copies[2].wait()
    copies[3].wait()


def margin_kernel(number, plan_ref, values, coupling_ref, *refs):
    *so_far, out_ref, picked = refs
    product = margin_product(number, plan_ref, values, coupling_ref, picked)
    out_ref[...] = so_far[0][...] + product if so_far else product


def last_kernel(numbers, scale, plan_ref, table_ref, turned_ref, first_ref, so_far, *refs):
    arrived = refs[: len(numbers)]
    coupling_ref, inverse_ref, stiffness_ref, out_ref, picked, margin = refs[len(numbers) :]
    columns = margin.shape[0]
    for at, (number, values) in enumerate(zip(numbers, arrived)):
        product = margin_product(number, plan_ref, values, coupling_ref, picked)
        margin[...] = (so_far if at == 0 else margin)[...] + product
    extension = (
        first_ref[...]
        + jnp.dot(margin[...].astype(BF16), inverse_ref[...], preferred_element_type=F32)
    ).astype(BF16)
    projected = jnp.dot(extension, stiffness_ref[...], preferred_element_type=F32).astype(BF16)
    coarse = lax.dot_general(
        projected, extension, (((1,), (1,)), ((), ())), preferred_element_type=F32
    )
    coarse = (coarse * scale).astype(BF16)
    placed = jnp.dot(table_ref[...], coarse, preferred_element_type=F32).astype(BF16)
    out_ref[...] = jnp.dot(placed, turned_ref[...], preferred_element_type=F32).astype(BF16)


def shards(swaps, sources, basis, stiffness, inverse, coupling, panel_index, panel_count, owner_map):
    basis, stiffness, inverse, coupling = (a[0, 0] for a in (basis, stiffness, inverse, coupling))
    columns, rows = basis.shape
    blocks = lax.axis_size("grp") * lax.axis_size("sub")
    columns_all = OWN * blocks
    arrivals = [None] * len(swaps)
    for number in ORDER:
        arrivals[number] = lax.ppermute(basis, ("grp", "sub"), swaps[number])
    stay = lambda *arrays: tuple(pltpu.with_memory_space_constraint(a, pltpu.HBM) for a in arrays)
    tables = stay(jnp.asarray(sources), panel_index, panel_count)
    scale = float(rows * columns) ** -0.5
    slots_wide = coupling.shape[1]
    picked = pltpu.VMEM((columns, slots_wide), BF16)
    step = 2 * columns * slots_wide * rows
    room = 8 * 2**20 + 4 * columns_all**2
    params = pltpu.CompilerParams(vmem_limit_bytes=room)
    whole = jax.ShapeDtypeStruct((columns, rows), F32)
    plan, first, table, turned, inverse, coupling, stiffness = pl.pallas_call(
        early_kernel,
        out_shape=(
            jax.ShapeDtypeStruct((8, 128), jnp.int32),
            whole,
            jax.ShapeDtypeStruct((columns_all, columns), BF16),
            jax.ShapeDtypeStruct((columns, columns_all), BF16),
            *(jax.ShapeDtypeStruct(a.shape, BF16) for a in (inverse, coupling, stiffness)),
        ),
        in_specs=[SMEM] * 3 + [VMEM] + [HBM] * 4,
        out_specs=(VMEM,) * 7,
        scratch_shapes=[
            pltpu.VMEM((columns, rows), BF16), pltpu.SemaphoreType.DMA((4,))
        ],
        cost_estimate=pl.CostEstimate(
            flops=2 * columns * rows * rows, bytes_accessed=26 * 2**20, transcendentals=0
        ),
        compiler_params=pltpu.CompilerParams(vmem_limit_bytes=room + 16 * 2**20),
    )(*tables, *stay(owner_map, basis, inverse, coupling, stiffness))
    margin = ()
    for number in MIDDLE:
        margin = (
            pl.pallas_call(
                lambda *refs, number=number: margin_kernel(number, *refs),
                out_shape=whole,
                in_specs=[VMEM] * (3 + len(margin)),
                out_specs=VMEM,
                scratch_shapes=[picked],
                cost_estimate=pl.CostEstimate(
                    flops=step, bytes_accessed=3 * 2**20, transcendentals=0
                ),
                compiler_params=params,
            )(plan, arrivals[number], coupling, *margin),
        )
    contributions = pl.pallas_call(
        lambda *refs: last_kernel(LATE, scale, *refs),
        out_shape=jax.ShapeDtypeStruct((columns_all, columns_all), BF16),
        in_specs=[VMEM] * (8 + len(LATE)),
        out_specs=VMEM,
        scratch_shapes=[picked, pltpu.VMEM((columns, rows), F32)],
        cost_estimate=pl.CostEstimate(
            flops=step * len(LATE) + 2 * columns * rows * (2 * rows + columns),
            bytes_accessed=12 * 2**20,
            transcendentals=0,
        ),
        compiler_params=params,
    )(plan, table, turned, first, *margin, *(arrivals[n] for n in LATE), coupling, inverse, stiffness)
    parts = lax.all_to_all(
        contributions.reshape(blocks, OWN, columns_all), ("grp", "sub"), 0, 0, tiled=True
    )
    return jnp.sum(parts.astype(F32), axis=0)


def solution(mesh):
    three, four = P("grp", "sub", None), P("grp", "sub", None, None)
    in_specs = (four, four, four, P("grp", "sub", None, None, None), four, three, three)
    out_specs = P(("grp", "sub"), None)
    swaps, sources = exchange_rounds(mesh.shape["grp"], mesh.shape["sub"])
    return jax.shard_map(
        lambda *args: shards(swaps, sources, *args),
        mesh=mesh, in_specs=in_specs, out_specs=out_specs, check_vma=False,
    )
```

```python
import jax
import jax.numpy as jnp
import numpy as np
from jax import lax
from jax.experimental import pallas as pl
from jax.experimental.pallas import tpu as pltpu
from jax.sharding import PartitionSpec as P

PANEL = 128
OWN = 8
F32 = jnp.float32
BF16 = jnp.bfloat16
FIRST, MIDDLE, LATE = (3, 0), 1, 2
ORDER = (0, 1, 2, 3)
VMEM = pl.BlockSpec(memory_space=pltpu.VMEM)
SMEM = pl.BlockSpec(memory_space=pltpu.SMEM)
HBM = pl.BlockSpec(memory_space=pltpu.HBM)


def exchange_rounds(groups, members):
    rounds = [[], [], [], []]
    for g in range(groups):
        inner = g % 4 in (1, 2)
        across = g + 1 < groups if g % 2 else g > 0
        turns = ("BXA" if inner else "ABX") if across else "AB"
        for s in range(members - 1):
            rounds[turns.index("BA"[s % 2 == 0])].append(((g, s), (g, s + 1)))
        if g + 1 < groups:
            for s in range(members):
                if g % 2 == 0:
                    number = 3
                elif s == 0 or s == members - 1 and s % 2:
                    number = min({0, 1, 2} - {turns.index("A")})
                else:
                    number = turns.index("X")
                rounds[number].append(((g, s), (g + 1, s)))
    sources = np.full((groups * members, len(rounds)), -1, np.int32)
    swaps = []
    for number, pairs in enumerate(rounds):
        flat = []
        for low, high in pairs:
            a, b = (g * members + s for g, s in (low, high))
            along_sub = low[0] == high[0]
            assert max(sources[a, number], sources[b, number]) < 0
            sources[a, number] = 3 if along_sub else 1
            sources[b, number] = 2 if along_sub else 0
            flat += [(a, b), (b, a)]
        swaps.append(flat)
    return swaps, sources


def packing(panels, slots):
    bits, count_bits = (panels - 1).bit_length(), slots.bit_length()
    assert slots * bits + count_bits + 2 < 32
    return bits, count_bits


def unpacked(number, plan_ref, panels, slots):
    bits, count_bits = packing(panels, slots)
    plan = plan_ref[0, number]
    places = [(plan >> (2 + count_bits + slot * bits)) & (2**bits - 1) for slot in range(slots)]
    return plan & 3, (plan >> 2) & (2**count_bits - 1), places


def side_by_side(values, live, places):
    panels = []
    for slot, place in enumerate(places):
        panel = values[:, pl.ds(pl.multiple_of(place * PANEL, PANEL), PANEL)]
        panels.append(panel * jnp.where(slot < live, 1.0, 0.0).astype(BF16))
    return jnp.concatenate(panels, axis=1)


def margin_product(number, plan_ref, values, coupling_ref):
    panels, slots = (width // PANEL for width in (values.shape[1], coupling_ref.shape[1]))
    direction, live, places = unpacked(number, plan_ref, panels, slots)
    return jnp.dot(
        side_by_side(values, live, places), coupling_ref[direction], preferred_element_type=F32
    )


def write_plans(source_ref, index_ref, count_ref, panels, plan_ref):
    slots = index_ref.shape[-1]
    bits, count_bits = packing(panels, slots)
    me = place_of()
    at = lax.broadcasted_iota(jnp.int32, plan_ref.shape, 1)
    plans = jnp.zeros(plan_ref.shape, jnp.int32)
    for number in range(source_ref.shape[1]):
        source = source_ref[me, number]
        direction = jnp.maximum(source, 0)
        plan = direction + jnp.where(source < 0, 0, count_ref[0, 0, direction]) * 4
        for slot in range(slots):
            plan += index_ref[0, 0, direction, slot] << (2 + count_bits + slot * bits)
        plans = jnp.where(at == number, plan, plans)
    plan_ref[...] = plans


def place_of():
    return lax.axis_index("grp") * lax.axis_size("sub") + lax.axis_index("sub")


def early_kernel(
    source_ref, index_ref, count_ref, owner_ref, basis_hbm, inverse_hbm, coupling_hbm, stiffness_hbm,
    plan_ref, first_ref, table_ref, turned_ref, through_ref, inverse_ref, coupling_ref, stiffness_ref,
    basis_ref, arrived,
):
    last = jnp.maximum(source_ref[place_of(), LATE], 0)
    pairs = [(inverse_hbm, inverse_ref)]
    pairs += [(coupling_hbm.at[last ^ way], coupling_ref.at[last ^ way]) for way in range(4)]
    pairs[2:2] = [(basis_hbm, basis_ref)]
    pairs += [(stiffness_hbm, stiffness_ref)]
    copies = [
        pltpu.make_async_copy(source, target, arrived.at[at])
        for at, (source, target) in enumerate(pairs)
    ]
    for copy in copies:
        copy.start()
    write_plans(source_ref, index_ref, count_ref, basis_ref.shape[1] // PANEL, plan_ref)
    places = lax.broadcasted_iota(jnp.int32, table_ref.shape, 0)
    table = (owner_ref[0] == places).astype(F32)
    table_ref[...] = table.astype(BF16)
    turned_ref[...] = table.T.astype(BF16)
    copies[0].wait()
    copies[1].wait()
    depth = through_ref.shape[0]
    part = 2 * PANEL if depth % (2 * PANEL) == 0 else PANEL
    for start in range(0, depth, part):
        through_ref[start : start + part] = jnp.dot(
            coupling_ref[last, start : start + part], inverse_ref[...], preferred_element_type=F32
        ).astype(BF16)
    copies[2].wait()
    first_ref[...] = jnp.dot(basis_ref[...], inverse_ref[...], preferred_element_type=F32)
    for copy in copies[3:]:
        copy.wait()


def margin_kernel(number, plan_ref, values, coupling_ref, *refs):
    *so_far, out_ref = refs
    product = margin_product(number, plan_ref, values, coupling_ref)
    out_ref[...] = so_far[0][...] + product if so_far else product


def partial_kernel(number, plan_ref, values, coupling_ref, so_far, first_ref, inverse_ref, out_ref):
    margin = so_far[...] + margin_product(number, plan_ref, values, coupling_ref)
    out_ref[...] = first_ref[...] + jnp.dot(
        margin.astype(BF16), inverse_ref[...], preferred_element_type=F32
    )


def last_kernel(
    scale, plan_ref, table_ref, turned_ref, partial_ref, values, through_ref, stiffness_ref,
    out_ref, extension_ref,
):
    panels, slots = (width // PANEL for width in (values.shape[1], through_ref.shape[0]))
    _, live, places = unpacked(LATE, plan_ref, panels, slots)

    @pl.when(live == 0)
    def _():
        extension_ref[...] = partial_ref[...].astype(BF16)

    @pl.when(live > 0)
    def _():
        picked = side_by_side(values, live, places)
        product = jnp.dot(picked, through_ref[...], preferred_element_type=F32)
        extension_ref[...] = (partial_ref[...] + product).astype(BF16)

    extension = extension_ref[...]
    projected = jnp.dot(extension, stiffness_ref[...], preferred_element_type=F32).astype(BF16)
    coarse = lax.dot_general(
        projected, extension, (((1,), (1,)), ((), ())), preferred_element_type=F32
    )
    coarse = (coarse * scale).astype(BF16)
    placed = jnp.dot(table_ref[...], coarse, preferred_element_type=F32).astype(BF16)
    out_ref[...] = jnp.dot(placed, turned_ref[...], preferred_element_type=F32).astype(BF16)


def shards(swaps, sources, basis, stiffness, inverse, coupling, panel_index, panel_count, owner_map):
    basis, stiffness, inverse, coupling = (a[0, 0] for a in (basis, stiffness, inverse, coupling))
    columns, rows = basis.shape
    blocks = lax.axis_size("grp") * lax.axis_size("sub")
    columns_all = OWN * blocks
    arrivals = [None] * len(swaps)
    for number in ORDER:
        arrivals[number] = lax.ppermute(basis, ("grp", "sub"), swaps[number])
    stay = lambda *arrays: tuple(pltpu.with_memory_space_constraint(a, pltpu.HBM) for a in arrays)
    tables = stay(jnp.asarray(sources), panel_index, panel_count)
    scale = float(rows * columns) ** -0.5
    slots_wide = coupling.shape[1]
    step = 2 * columns * slots_wide * rows
    room = 8 * 2**20 + 4 * columns_all**2
    params = pltpu.CompilerParams(vmem_limit_bytes=room)
    whole = jax.ShapeDtypeStruct((columns, rows), F32)
    plan, first, table, turned, through, inverse, coupling, stiffness = pl.pallas_call(
        early_kernel,
        out_shape=(
            jax.ShapeDtypeStruct((8, 128), jnp.int32),
            whole,
            jax.ShapeDtypeStruct((columns_all, columns), BF16),
            jax.ShapeDtypeStruct((columns, columns_all), BF16),
            jax.ShapeDtypeStruct((slots_wide, rows), BF16),
            *(jax.ShapeDtypeStruct(a.shape, BF16) for a in (inverse, coupling, stiffness)),
        ),
        in_specs=[SMEM] * 3 + [VMEM] + [HBM] * 4,
        out_specs=(VMEM,) * 8,
        scratch_shapes=[
            pltpu.VMEM((columns, rows), BF16), pltpu.SemaphoreType.DMA((7,))
        ],
        cost_estimate=pl.CostEstimate(
            flops=2 * (columns + slots_wide) * rows * rows, bytes_accessed=26 * 2**20, transcendentals=0
        ),
        compiler_params=pltpu.CompilerParams(vmem_limit_bytes=room + 16 * 2**20),
    )(*tables, *stay(owner_map, basis, inverse, coupling, stiffness))
    margin = ()
    for number in FIRST:
        margin = (
            pl.pallas_call(
                lambda *refs, number=number: margin_kernel(number, *refs),
                out_shape=whole,
                in_specs=[VMEM] * (3 + len(margin)),
                out_specs=VMEM,
                cost_estimate=pl.CostEstimate(
                    flops=step, bytes_accessed=3 * 2**20, transcendentals=0
                ),
                compiler_params=params,
            )(plan, arrivals[number], coupling, *margin),
        )
    partial = pl.pallas_call(
        lambda *refs: partial_kernel(MIDDLE, *refs),
        out_shape=whole,
        in_specs=[VMEM] * 6,
        out_specs=VMEM,
        cost_estimate=pl.CostEstimate(
            flops=step + 2 * columns * rows * rows, bytes_accessed=6 * 2**20, transcendentals=0
        ),
        compiler_params=params,
    )(plan, arrivals[MIDDLE], coupling, *margin, first, inverse)
    contributions = pl.pallas_call(
        lambda *refs: last_kernel(scale, *refs),
        out_shape=jax.ShapeDtypeStruct((columns_all, columns_all), BF16),
        in_specs=[VMEM] * 7,
        out_specs=VMEM,
        scratch_shapes=[pltpu.VMEM((columns, rows), BF16)],
        cost_estimate=pl.CostEstimate(
            flops=step + 2 * columns * rows * (rows + columns),
            bytes_accessed=8 * 2**20,
            transcendentals=0,
        ),
        compiler_params=params,
    )(plan, table, turned, partial, arrivals[LATE], through, stiffness)
    parts = lax.all_to_all(
        contributions.reshape(blocks, OWN, columns_all), ("grp", "sub"), 0, 0, tiled=True
    )
    return jnp.sum(parts.astype(F32), axis=0)


def solution(mesh):
    three, four = P("grp", "sub", None), P("grp", "sub", None, None)
    in_specs = (four, four, four, P("grp", "sub", None, None, None), four, three, three)
    out_specs = P(("grp", "sub"), None)
    swaps, sources = exchange_rounds(mesh.shape["grp"], mesh.shape["sub"])
    return jax.shard_map(
        lambda *args: shards(swaps, sources, *args),
        mesh=mesh, in_specs=in_specs, out_specs=out_specs, check_vma=False,
    )
```

```python
import jax
import jax.numpy as jnp
import numpy as np
from jax import lax
from jax.experimental import pallas as pl
from jax.experimental.pallas import tpu as pltpu
from jax.sharding import PartitionSpec as P

PANEL = 128
OWN = 8
F32 = jnp.float32
BF16 = jnp.bfloat16
FIRST, MIDDLE, LATE = (3, 0), 1, 2
ORDER = (0, 1, 2, 3)
VMEM = pl.BlockSpec(memory_space=pltpu.VMEM)
SMEM = pl.BlockSpec(memory_space=pltpu.SMEM)
HBM = pl.BlockSpec(memory_space=pltpu.HBM)


def exchange_rounds(groups, members):
    rounds = [[], [], [], []]
    for g in range(groups):
        inner = g % 4 in (1, 2)
        across = g + 1 < groups if g % 2 else g > 0
        turns = ("BXA" if inner else "ABX") if across else "AB"
        for s in range(members - 1):
            rounds[turns.index("BA"[s % 2 == 0])].append(((g, s), (g, s + 1)))
        if g + 1 < groups:
            for s in range(members):
                if g % 2 == 0:
                    number = 3
                elif s == 0 or s == members - 1 and s % 2:
                    number = min({0, 1, 2} - {turns.index("A")})
                else:
                    number = turns.index("X")
                rounds[number].append(((g, s), (g + 1, s)))
    sources = np.full((groups * members, len(rounds)), -1, np.int32)
    swaps = []
    for number, pairs in enumerate(rounds):
        flat = []
        for low, high in pairs:
            a, b = (g * members + s for g, s in (low, high))
            along_sub = low[0] == high[0]
            assert max(sources[a, number], sources[b, number]) < 0
            sources[a, number] = 3 if along_sub else 1
            sources[b, number] = 2 if along_sub else 0
            flat += [(a, b), (b, a)]
        swaps.append(flat)
    return swaps, sources


def packing(panels, slots):
    bits, count_bits = (panels - 1).bit_length(), slots.bit_length()
    assert slots * bits + count_bits + 2 < 32
    return bits, count_bits


def unpacked(number, plan_ref, panels, slots):
    bits, count_bits = packing(panels, slots)
    plan = plan_ref[0, number]
    places = [(plan >> (2 + count_bits + slot * bits)) & (2**bits - 1) for slot in range(slots)]
    return plan & 3, (plan >> 2) & (2**count_bits - 1), places


def side_by_side(values, live, places):
    panels = []
    for slot, place in enumerate(places):
        panel = values[:, pl.ds(pl.multiple_of(place * PANEL, PANEL), PANEL)]
        panels.append(panel * jnp.where(slot < live, 1.0, 0.0).astype(BF16))
    return jnp.concatenate(panels, axis=1)


def margin_product(number, plan_ref, values, coupling_ref):
    panels, slots = (width // PANEL for width in (values.shape[1], coupling_ref.shape[1]))
    direction, live, places = unpacked(number, plan_ref, panels, slots)
    return jnp.dot(
        side_by_side(values, live, places), coupling_ref[direction], preferred_element_type=F32
    )


def write_plans(source_ref, index_ref, count_ref, panels, plan_ref):
    slots = index_ref.shape[-1]
    bits, count_bits = packing(panels, slots)
    me = place_of()
    at = lax.broadcasted_iota(jnp.int32, plan_ref.shape, 1)
    plans = jnp.zeros(plan_ref.shape, jnp.int32)
    for number in range(source_ref.shape[1]):
        source = source_ref[me, number]
        direction = jnp.maximum(source, 0)
        plan = direction + jnp.where(source < 0, 0, count_ref[0, 0, direction]) * 4
        for slot in range(slots):
            plan += index_ref[0, 0, direction, slot] << (2 + count_bits + slot * bits)
        plans = jnp.where(at == number, plan, plans)
    plan_ref[...] = plans


def place_of():
    return lax.axis_index("grp") * lax.axis_size("sub") + lax.axis_index("sub")


def early_kernel(
    source_ref, index_ref, count_ref, owner_ref, basis_hbm, inverse_hbm, coupling_hbm, stiffness_hbm,
    plan_ref, first_ref, table_ref, turned_ref, through_ref, inverse_ref, coupling_ref, stiffness_ref,
    basis_ref, arrived,
):
    last = jnp.maximum(source_ref[place_of(), LATE], 0)
    pairs = [(inverse_hbm, inverse_ref)]
    pairs += [(coupling_hbm.at[last ^ way], coupling_ref.at[last ^ way]) for way in range(4)]
    pairs[2:2] = [(basis_hbm, basis_ref)]
    pairs += [(stiffness_hbm, stiffness_ref)]
    copies = [
        pltpu.make_async_copy(source, target, arrived.at[at])
        for at, (source, target) in enumerate(pairs)
    ]
    for copy in copies:
        copy.start()
    write_plans(source_ref, index_ref, count_ref, basis_ref.shape[1] // PANEL, plan_ref)
    places = lax.broadcasted_iota(jnp.int32, table_ref.shape, 0)
    table = (owner_ref[0] == places).astype(F32)
    table_ref[...] = table.astype(BF16)
    turned_ref[...] = table.T.astype(BF16)
    copies[0].wait()
    copies[1].wait()
    depth = through_ref.shape[0]
    part = 2 * PANEL if depth % (2 * PANEL) == 0 else PANEL
    for start in range(0, depth, part):
        through_ref[start : start + part] = jnp.dot(
            coupling_ref[last, start : start + part], inverse_ref[...], preferred_element_type=F32
        ).astype(BF16)
    copies[2].wait()
    first_ref[...] = jnp.dot(basis_ref[...], inverse_ref[...], preferred_element_type=F32)
    for copy in copies[3:]:
        copy.wait()


def margin_kernel(number, plan_ref, values, coupling_ref, *refs):
    *so_far, out_ref = refs
    product = margin_product(number, plan_ref, values, coupling_ref)
    out_ref[...] = so_far[0][...] + product if so_far else product


def partial_kernel(number, plan_ref, values, coupling_ref, so_far, first_ref, inverse_ref, out_ref):
    margin = so_far[...] + margin_product(number, plan_ref, values, coupling_ref)
    out_ref[...] = first_ref[...] + jnp.dot(
        margin.astype(BF16), inverse_ref[...], preferred_element_type=F32
    )


def last_kernel(
    scale, plan_ref, table_ref, turned_ref, partial_ref, values, through_ref, stiffness_ref,
    out_ref, extension_ref,
):
    panels, slots = (width // PANEL for width in (values.shape[1], through_ref.shape[0]))
    _, live, places = unpacked(LATE, plan_ref, panels, slots)

    @pl.when(live == 0)
    def _():
        extension_ref[...] = partial_ref[...].astype(BF16)

    @pl.when(live > 0)
    def _():
        picked = side_by_side(values, live, places)
        product = jnp.dot(picked, through_ref[...], preferred_element_type=F32)
        extension_ref[...] = (partial_ref[...] + product).astype(BF16)

    extension = extension_ref[...]
    projected = jnp.dot(extension, stiffness_ref[...], preferred_element_type=F32).astype(BF16)
    coarse = lax.dot_general(
        projected, extension, (((1,), (1,)), ((), ())), preferred_element_type=F32
    )
    coarse = (coarse * scale).astype(BF16)
    placed = jnp.dot(table_ref[...], coarse, preferred_element_type=F32).astype(BF16)
    out_ref[...] = jnp.dot(placed, turned_ref[...], preferred_element_type=F32).astype(BF16)


def shards(swaps, sources, basis, stiffness, inverse, coupling, panel_index, panel_count, owner_map):
    basis, stiffness, inverse, coupling = (a[0, 0] for a in (basis, stiffness, inverse, coupling))
    columns, rows = basis.shape
    blocks = lax.axis_size("grp") * lax.axis_size("sub")
    columns_all = OWN * blocks
    arrivals = [None] * len(swaps)
    for number in ORDER:
        arrivals[number] = lax.ppermute(basis, ("grp", "sub"), swaps[number])
    stay = lambda *arrays: tuple(pltpu.with_memory_space_constraint(a, pltpu.HBM) for a in arrays)
    tables = stay(jnp.asarray(sources), panel_index, panel_count)
    scale = float(rows * columns) ** -0.5
    slots_wide = coupling.shape[1]
    step = 2 * columns * slots_wide * rows
    room = 8 * 2**20 + 4 * columns_all**2
    params = pltpu.CompilerParams(vmem_limit_bytes=room)
    whole = jax.ShapeDtypeStruct((columns, rows), F32)
    plan, first, table, turned, through, inverse, coupling, stiffness = pl.pallas_call(
        early_kernel,
        out_shape=(
            jax.ShapeDtypeStruct((8, 128), jnp.int32),
            whole,
            jax.ShapeDtypeStruct((columns_all, columns), BF16),
            jax.ShapeDtypeStruct((columns, columns_all), BF16),
            jax.ShapeDtypeStruct((slots_wide, rows), BF16),
            *(jax.ShapeDtypeStruct(a.shape, BF16) for a in (inverse, coupling, stiffness)),
        ),
        in_specs=[SMEM] * 3 + [VMEM] + [HBM] * 4,
        out_specs=(VMEM,) * 8,
        scratch_shapes=[
            pltpu.VMEM((columns, rows), BF16), pltpu.SemaphoreType.DMA((7,))
        ],
        cost_estimate=pl.CostEstimate(
            flops=2 * (columns + slots_wide) * rows * rows, bytes_accessed=26 * 2**20, transcendentals=0
        ),
        compiler_params=pltpu.CompilerParams(vmem_limit_bytes=room + 16 * 2**20),
    )(*tables, *stay(owner_map, basis, inverse, coupling, stiffness))
    margin = ()
    for number in FIRST:
        margin = (
            pl.pallas_call(
                lambda *refs, number=number: margin_kernel(number, *refs),
                out_shape=whole,
                in_specs=[VMEM] * (3 + len(margin)),
                out_specs=VMEM,
                cost_estimate=pl.CostEstimate(
                    flops=step, bytes_accessed=3 * 2**20, transcendentals=0
                ),
                compiler_params=params,
            )(plan, arrivals[number], coupling, *margin),
        )
    partial = pl.pallas_call(
        lambda *refs: partial_kernel(MIDDLE, *refs),
        out_shape=whole,
        in_specs=[VMEM] * 6,
        out_specs=VMEM,
        cost_estimate=pl.CostEstimate(
            flops=step + 2 * columns * rows * rows, bytes_accessed=6 * 2**20, transcendentals=0
        ),
        compiler_params=pltpu.CompilerParams(
            vmem_limit_bytes=room
        ),
    )(plan, arrivals[MIDDLE], coupling, *margin, first, inverse)
    contributions = pl.pallas_call(
        lambda *refs: last_kernel(scale, *refs),
        out_shape=jax.ShapeDtypeStruct((columns_all, columns_all), BF16),
        in_specs=[VMEM] * 7,
        out_specs=VMEM,
        scratch_shapes=[pltpu.VMEM((columns, rows), BF16)],
        cost_estimate=pl.CostEstimate(
            flops=step + 2 * columns * rows * (rows + columns),
            bytes_accessed=8 * 2**20,
            transcendentals=0,
        ),
        compiler_params=pltpu.CompilerParams(
            vmem_limit_bytes=room
        ),
    )(plan, table, turned, partial, arrivals[LATE], through, stiffness)
    parts = lax.all_to_all(
        contributions.reshape(blocks, OWN, columns_all), ("grp", "sub"), 0, 0, tiled=True
    )
    return jnp.sum(parts.astype(F32), axis=0)


def solution(mesh):
    three, four = P("grp", "sub", None), P("grp", "sub", None, None)
    in_specs = (four, four, four, P("grp", "sub", None, None, None), four, three, three)
    out_specs = P(("grp", "sub"), None)
    swaps, sources = exchange_rounds(mesh.shape["grp"], mesh.shape["sub"])
    return jax.shard_map(
        lambda *args: shards(swaps, sources, *args),
        mesh=mesh, in_specs=in_specs, out_specs=out_specs, check_vma=False,
    )
```
